32 devices in a mesh: ctx: 8 (over y, x, core), head: 4 (over z).
Axes of the slice: x: 2, y: 2, z: 4, core: 2. Of those that a mesh axis runs over, the one named last changes fastest.
Arguments:
- branch_rows: bfloat16 [4096, 2048], P(('ctx', 'head')), may hold values from -6 to 6
- expert_ids: int32 [4096, 8], P(('ctx', 'head')), may hold values from 0 to 31, all different within a row; in each aligned block of 128 rows (0 to 127, 128 to 255, ...) at most 48 rows name the same one
- targets: int32 [4096], P(('ctx', 'head')), may hold values from 0 to 4095, as said below
- router: bfloat16 [2048, 32], replicated, may hold values from -0.046875 to 0.046875
- w_gate: bfloat16 [32, 2048, 768], P(('ctx', 'head')), may hold values from -0.125 to 0.125
- w_up: bfloat16 [32, 2048, 768], P(('ctx', 'head')), may hold values from -0.125 to 0.125
- w_down: bfloat16 [32, 768, 2048], P(('ctx', 'head')), may hold values from -0.3125 to 0.3125
- stream: bfloat16 [4096, 2048], P('ctx', 'head'), may hold values from -6 to 6
- attn_gain: float32 [2048], replicated, may hold values from 0.1 to 1.9
- q_gain: float32 [4096], P('head'), may hold values from 0.5 to 7
- k_gain: float32 [512], replicated, may hold values from 0.8 to 6
- w_query: bfloat16 [2048, 4096], P(None, 'head')
- w_key: bfloat16 [2048, 512], replicated
- w_value: bfloat16 [2048, 512], replicated, may hold values from -0.125 to 0.125
- w_out: bfloat16 [4096, 2048], P('head'), may hold values from -0.375 to 0.375
Outputs:
- layer_out: bfloat16 [4096, 2048], P('ctx', 'head')
The draws below stay inside these ranges and needn't reach their ends.
Inputs may be any that keep to these rules, and one draw needn't show every extreme that they name: `expert_ids`: in each device's 128 rows no expert is named more than 48 times. `targets`: each device's 128 rows name exactly 16 positions in each block of 512 joined positions; positions may repeat.
All inputs are finite; a program needn't handle non-finite values.
Results may differ from the reference program's by a relative error of at most 0.018.
Values may be sent and summed in bfloat16 or wider, within the bound.
A program may use at most 192 MiB of HBM per device.

```python
import math
import jax
import jax.numpy as jnp
import numpy as np
from jax import lax

D = 2048
FF = 768
TOP = 8
QH = 32
KVH = 4
HD = 128
ROWS_DEV = 128
TOKC = 512
EXPERTS = 32
ROWS = 4096
SEQ = 4096
CAP = 48
RPO = 16
N_CTX = 8
N_HEAD = 4


def draw_targets(key, part):
    blocks = ROWS // ROWS_DEV
    owners = SEQ // TOKC
    spots = jax.random.randint(jax.random.fold_in(key, 11), (blocks, owners, RPO), 0, TOKC, dtype=jnp.int32)
    offsets = (jnp.arange(owners, dtype=jnp.int32) * TOKC)[None, :, None]
    placed = (spots + offsets).reshape(blocks, ROWS_DEV)
    block_keys = jax.random.split(jax.random.fold_in(key, 12), blocks)
    orders = jax.vmap(lambda block_key: jax.random.permutation(block_key, ROWS_DEV))(block_keys)
    return jnp.take_along_axis(placed, orders, 1).reshape(ROWS).astype(jnp.int32)


def query_key_pair(key):
    query_part = jax.random.truncated_normal(jax.random.fold_in(key, 21), -6.0, 6.0, (D, QH * HD), jnp.float32) / math.sqrt(D)
    key_part = jax.random.truncated_normal(jax.random.fold_in(key, 22), -6.0, 6.0, (D, KVH * HD), jnp.float32) / math.sqrt(D)
    return (query_part, key_part)


def draw_w_query(key, part):
    return query_key_pair(key)[0].astype(jnp.bfloat16)


def draw_w_key(key, part):
    return query_key_pair(key)[1].astype(jnp.bfloat16)


def draw_q_gain(key, part):
    return jnp.exp(jax.random.uniform(jax.random.fold_in(key, 33), (QH * HD,), jnp.float32, math.log(0.8), math.log(2.0)))


def draw_k_gain(key, part):
    return jnp.exp(jax.random.uniform(jax.random.fold_in(key, 42), (KVH * HD,), jnp.float32, math.log(0.8), math.log(2.0)))


def block_scale(rng, shape, pieces, low, largest):
    gain, own = 1.0, jax.random.fold_in(rng, 6)
    for position, shards_of in pieces:
        heights = jnp.exp(jax.random.uniform(jax.random.fold_in(own, position), (shards_of,), jnp.float32, low / len(pieces), largest / len(pieces)))
        gain = gain * jnp.repeat(heights, shape[position] // shards_of).reshape([-1 if axis == position else 1 for axis in range(len(shape))])
    return gain


def shared_out(rng, own, number, rows, number_of, top, reach, slope):
    sequence = jax.random.permutation(rng, number_of)
    packed, usual = portions_of(number_of, rows * top, reach, slope, True), portions_of(number_of, rows * top, reach, slope, False)
    places = jnp.arange(number_of)

    def named(tallies, offset_by):
        used = int((tallies > 0).sum())
        fixed = max(1, used // 4)
        passed = fixed + (places - fixed + offset_by * (used - fixed)) % max(1, number_of - fixed)
        return jnp.zeros((number_of,), jnp.int32).at[sequence[jnp.where(places < fixed, places, passed)]].set(jnp.asarray(tallies, jnp.int32))

    tallies = jnp.where(number % 4 == 0, named(packed, number // 4), named(usual, number - number // 4 - 1))
    mixed = jax.random.permutation(jax.random.fold_in(own, 3), number_of)
    donor, sink = mixed[0:number_of // 2 * 2:2], mixed[1:number_of // 2 * 2:2]
    slack = jnp.minimum(tallies[donor] - 1, reach - tallies[sink]) // 2
    slack = jnp.where((donor == sequence[0]) | (sink == sequence[0]) | (tallies[sink] == 0), 0, jnp.maximum(slack, 0))
    passed = jax.random.randint(jax.random.fold_in(own, 4), (number_of // 2,), 0, 1 << 20) % (slack + 1)
    tallies = tallies.at[donor].add(-passed).at[sink].add(passed)
    members = jnp.searchsorted(jnp.cumsum(tallies), jnp.arange(rows * top), side="right").astype(jnp.int32)
    listing = members.reshape(top, rows).T
    listing = listing[jax.random.permutation(jax.random.fold_in(own, 1), rows)]
    offset_by = jax.random.randint(jax.random.fold_in(own, 2), (rows, 1), 0, top)
    return jnp.take_along_axis(listing, (jnp.arange(top)[None, :] + offset_by) % top, axis=1)


def portions_of(number_of, total, most, slope, full):
    weights = [(1 << 20) // math.isqrt(standing ** slope) + 1 for standing in range(1, number_of + 1)]
    largest = most if full else min(most, max(-(-total // number_of), total * weights[0] // sum(weights)))
    least = 1 if total - largest >= number_of - 1 else 0
    holding, rest = [largest] + [least] * (number_of - 1), total - largest - least * (number_of - 1)
    while rest > 0:
        candidates = [i for i in range(1, number_of) if holding[i] < largest] or [i for i in range(1, number_of) if holding[i] < most]
        mass, remaining = sum([weights[i] for i in candidates]), rest
        for i in candidates:
            more = min(most - holding[i], max(1, remaining * weights[i] // mass), rest)
            holding[i] = holding[i] + more
            rest = rest - more
    return np.array(holding)


def normal_values(stream_key, dims, spread, most, cuts=(), kind=jnp.bfloat16):
    entries = spread * jax.random.normal(stream_key, dims, jnp.float32)
    if cuts:
        entries = entries * block_scale(stream_key, dims, cuts, -0.22, 0.18)
    return jnp.clip(entries, -most, most).astype(kind)


def setup_inputs(seed: int = 0) -> dict:
    arg_keys = jax.random.split(jax.random.key(seed), 16)
    branch_rows = normal_values(arg_keys[0], (ROWS, D), 1.0, 6.0, ((0, 32),))
    expert_ids_keys = jax.random.split(jax.random.fold_in(arg_keys[1], 1), ROWS // ROWS_DEV)
    expert_ids_turns = jax.random.permutation(jax.random.fold_in(arg_keys[1], 3), ROWS // ROWS_DEV)
    expert_ids = jax.vmap(lambda own, number: shared_out(jax.random.fold_in(arg_keys[1], 2), own, number, ROWS_DEV, EXPERTS, TOP, CAP, 2))(expert_ids_keys, expert_ids_turns).reshape((ROWS, TOP))
    targets = draw_targets(jax.random.fold_in(arg_keys[15], 71), 0)
    router = normal_values(arg_keys[3], (D, EXPERTS), (8 * D) ** -0.5, 0.046875)
    w_gate = normal_values(arg_keys[4], (EXPERTS, D, FF), D ** -0.5, 0.125, ((0, 32),))
    w_up = normal_values(arg_keys[5], (EXPERTS, D, FF), D ** -0.5, 0.125, ((0, 32),))
    w_down = normal_values(arg_keys[6], (EXPERTS, FF, D), (FF // 2) ** -0.5, 0.3125, ((0, 32),))
    stream = normal_values(arg_keys[7], (SEQ, D), 1.0, 6.0, ((0, 8), (1, 4)))
    attn_gain = jnp.clip(1.0 + 0.18 * jax.random.normal(arg_keys[8], (D,), jnp.float32), 0.1, 1.9)
    q_gain = draw_q_gain(jax.random.fold_in(arg_keys[15], 71), 0)
    k_gain = draw_k_gain(jax.random.fold_in(arg_keys[15], 71), 0)
    w_query = draw_w_query(jax.random.fold_in(arg_keys[15], 71), 0)
    w_key = draw_w_key(jax.random.fold_in(arg_keys[15], 71), 0)
    w_value = normal_values(arg_keys[13], (D, KVH * HD), D ** -0.5, 0.125)
    w_out = normal_values(arg_keys[14], (QH * HD, D), (2 * HD) ** -0.5, 0.375, ((0, 4),))
    return dict(branch_rows=branch_rows, expert_ids=expert_ids, targets=targets, router=router, w_gate=w_gate, w_up=w_up, w_down=w_down, stream=stream, attn_gain=attn_gain, q_gain=q_gain, k_gain=k_gain, w_query=w_query, w_key=w_key, w_value=w_value, w_out=w_out)


EPSILON = 1e-06
THETA = 1000000.0

def rotary(vectors, positions):
    half_dim = vectors.shape[-1] // 2
    frequency = jnp.power(jnp.float32(THETA), -jnp.arange(half_dim, dtype=jnp.float32) * 2.0 / vectors.shape[-1])
    angles = positions.astype(jnp.float32)[:, None] * frequency[None, :]
    cosines = jnp.cos(angles)[:, None, :]
    sines = jnp.sin(angles)[:, None, :]
    front_part = vectors[..., :half_dim]
    back_part = vectors[..., half_dim:]
    return jnp.concatenate([front_part * cosines - back_part * sines, back_part * cosines + front_part * sines], -1)

def head_norm(vectors, scales):
    return vectors * lax.rsqrt(lax.optimization_barrier(jnp.mean(vectors * vectors, -1, keepdims=True)) + EPSILON) * scales

def expert_rows(inputs, gate_proj, up_proj, down_proj):
    gate_part = jnp.dot(inputs, gate_proj, preferred_element_type=jnp.float32)
    upward = jnp.dot(inputs, up_proj, preferred_element_type=jnp.float32)
    hidden = (jax.nn.silu(gate_part) * upward).astype(jnp.bfloat16)
    return jnp.dot(hidden, down_proj, preferred_element_type=jnp.float32).astype(jnp.bfloat16)

def slot_index(expert_block):
    flat_ids = expert_block.reshape(-1)
    onehot = (flat_ids[:, None] == jnp.arange(EXPERTS, dtype=jnp.int32)[None, :]).astype(jnp.int32)
    earlier = jnp.cumsum(onehot, 0) - onehot
    return lax.optimization_barrier(jnp.sum(earlier * onehot, 1)).astype(jnp.int32)

def reference(branch_rows, expert_ids, targets, router, w_gate, w_up, w_down, stream, attn_gain, q_gain, k_gain, w_query, w_key, w_value, w_out):
    devices = N_CTX * N_HEAD
    logits = jnp.dot(branch_rows, router, preferred_element_type=jnp.float32)
    chosen = expert_ids[:, :, None] == jnp.arange(EXPERTS, dtype=jnp.int32)[None, None, :]
    picked = lax.optimization_barrier(jnp.sum(jnp.where(chosen, logits[:, None, :], 0.0), -1))
    gate_probs = jax.nn.softmax(picked, -1)
    blocks = expert_ids.reshape(devices, ROWS_DEV, TOP)
    slots = jax.vmap(slot_index)(blocks)
    expert_flat = blocks.reshape(devices, ROWS_DEV * TOP)
    columns = (jnp.arange(devices, dtype=jnp.int32)[:, None] * CAP + slots).astype(jnp.int32)
    repeated = jnp.repeat(branch_rows, TOP, axis=0).reshape(devices, ROWS_DEV * TOP, D)
    buffer = jnp.zeros((EXPERTS, devices * CAP, D), jnp.bfloat16).at[expert_flat, columns].set(repeated)
    expert_out = lax.map(lambda operands: expert_rows(operands[0], operands[1], operands[2], operands[3]), (buffer, w_gate, w_up, w_down))
    gathered_out = expert_out[expert_flat, columns].reshape(ROWS, TOP, D)
    merged = jnp.zeros((ROWS, D), jnp.float32)
    for which in range(TOP):
        merged = merged + gate_probs[:, which, None] * gathered_out[:, which].astype(jnp.float32)
    merged = merged.astype(jnp.bfloat16)
    joined = stream.astype(jnp.float32).at[targets].add(merged.astype(jnp.float32)).astype(jnp.bfloat16)
    joined_f = joined.astype(jnp.float32)
    normed = (joined_f * lax.rsqrt(lax.optimization_barrier(jnp.mean(joined_f * joined_f, -1, keepdims=True)) + EPSILON) * attn_gain).astype(jnp.bfloat16)
    positions = jnp.arange(SEQ, dtype=jnp.int32)
    queries = jnp.dot(normed, w_query, preferred_element_type=jnp.float32).reshape(SEQ, QH, HD)
    queries = rotary(head_norm(queries, q_gain.reshape(QH, HD)), positions).astype(jnp.bfloat16)
    key_rows = jnp.dot(normed, w_key, preferred_element_type=jnp.float32).reshape(SEQ, KVH, HD)
    key_rows = rotary(head_norm(key_rows, k_gain.reshape(KVH, HD)), positions).astype(jnp.bfloat16)
    values = jnp.dot(normed, w_value, preferred_element_type=jnp.float32).astype(jnp.bfloat16).reshape(SEQ, KVH, HD)
    group_size = QH // KVH
    head_queries = queries.transpose(1, 0, 2)
    head_keys = jnp.repeat(key_rows.transpose(1, 0, 2), group_size, axis=0)
    head_values = jnp.repeat(values.transpose(1, 0, 2), group_size, axis=0)
    causal = positions[:, None] >= positions[None, :]

    def one_head(operands):
        scores = jnp.dot(operands[0], operands[1].T, preferred_element_type=jnp.float32) / math.sqrt(HD)
        highest = lax.optimization_barrier(jnp.max(jnp.where(causal, scores, -1e+30), -1))
        weights = jnp.where(causal, jnp.exp(scores - highest[:, None]), 0.0)
        totals = lax.optimization_barrier(jnp.sum(weights, -1))
        summed = jnp.dot(weights.astype(jnp.bfloat16), operands[2], preferred_element_type=jnp.float32)
        return (summed / totals[:, None]).astype(jnp.bfloat16)
    attended = lax.map(one_head, (head_queries, head_keys, head_values))
    attended = attended.transpose(1, 0, 2).reshape(SEQ, QH * HD)
    group_cols = QH * HD // N_HEAD
    projected = jnp.zeros((SEQ, D), jnp.float32)
    for group in range(N_HEAD):
        part_out = jnp.dot(attended[:, group * group_cols:(group + 1) * group_cols], w_out[group * group_cols:(group + 1) * group_cols], preferred_element_type=jnp.float32)
        rounded = lax.optimization_barrier(part_out.astype(jnp.bfloat16))
        projected = projected + rounded.astype(jnp.float32)
    layer_out = (joined_f + projected).astype(jnp.bfloat16)
    return layer_out
```

```python
import functools
import math

import jax
import jax.numpy as jnp
from jax import lax
from jax.experimental import pallas as pl
from jax.experimental.pallas import tpu as pltpu
from jax.sharding import PartitionSpec as P

QH = 32
KVH = 4
HD = 128

EPSILON = 1e-06
THETA = 1000000.0
BOTH = ("ctx", "head")


def rotary_tables(positions):
    half_dim = HD // 2
    frequency = jnp.power(
        jnp.float32(THETA), -jnp.arange(half_dim, dtype=jnp.float32) * 2.0 / HD
    )
    angles = positions.astype(jnp.float32)[:, None] * frequency[None, :]
    cosines = jnp.cos(angles)
    sines = jnp.sin(angles)
    return jnp.concatenate([cosines, cosines], -1), jnp.concatenate([-sines, sines], -1)


def exclusive_count(onehot):
    rows = onehot.shape[-2]
    lower = (jnp.arange(rows)[:, None] > jnp.arange(rows)[None, :]).astype(jnp.bfloat16)
    return jnp.einsum("rq,...qe->...re", lower, onehot, preferred_element_type=jnp.float32)


def split_ctx(ctx_count):
    low = 2 if ctx_count % 2 == 0 else 1
    middle = 2 if (ctx_count // low) % 2 == 0 else 1
    return ctx_count // (low * middle), middle, low


def choose(index, values):
    result = values[0]
    for i, value in enumerate(values[1:], 1):
        result = jnp.where(index == i, value, result)
    return result


def expert_kernel(
    ctx_count, heads, experts, rows, extra, capacity,
    own_ref, gate_hbm, up_hbm,
    gathered, hidden_ref,
    gate_w, up_w, block_ref, inputs, scales, weight_sem, load_sem, own_sem, send_sem, recv_sem, half_sem,
):
    U, V, W = split_ctx(ctx_count)
    ctx = lax.axis_index("ctx")
    h = lax.axis_index("head")
    u, v, w = ctx // (V * W), lax.rem(ctx // W, V), lax.rem(ctx, W)
    width = own_ref.shape[1]
    total = rows + extra
    cut = (total // 2) // 16 * 16
    mine = ctx * heads + h

    def block_of(uu, vv, ww, hh):
        return ((uu * V + vv) * W + ww) * heads + hh

    def ctx_of(uu, vv, ww):
        return (uu * V + vv) * W + ww

    xs = [lax.rem(v + i, V) for i in range(1, V)]
    ys = [lax.rem(u + i, U) for i in range(1, U)]
    ws = [lax.rem(w + i, W) for i in range(1, W)]
    lows = [h - s for s in range(heads)]
    highs = [h + s for s in range(heads)]
    peers = [({"ctx": ctx, "head": h - 1}, h > 0), ({"ctx": ctx, "head": h + 1}, h + 1 < heads)]
    peers += [({"ctx": ctx_of(u, x, w), "head": h}, None) for x in xs]
    peers += [({"ctx": ctx_of(y, v, w), "head": h}, None) for y in ys]
    peers += [({"ctx": ctx_of(u, v, s), "head": h}, None) for s in ws]

    def guarded(condition, action):
        if condition is None:
            action()
        else:
            pl.when(condition)(action)

    def both(first, second):
        if first is None:
            return second
        return first if second is None else first & second

    def span(half):
        if half is None:
            return slice(None)
        return pl.ds(0, cut) if half == 0 else pl.ds(cut, total - cut)

    def recv_of(block, half):
        return half_sem.at[block] if half == 1 else recv_sem.at[block]

    sends = []

    def plan(block, half, target, condition, own=False):
        sends.append((block, half, target, condition, own))
        return ("send", len(sends) - 1)

    def copy_of(index):
        block, half, target, condition, own = sends[index]
        source = own_ref if own else gathered.at[block, span(half)]
        return pltpu.make_async_remote_copy(
            src_ref=source,
            dst_ref=gathered.at[block, span(half)],
            send_sem=send_sem.at[index],
            recv_sem=recv_of(block, half),
            device_id=target,
            device_id_type=pl.DeviceIdType.MESH,
        )

    def wait_for(block, half, condition):
        return ("wait", block, half, condition)

    down = {"ctx": ctx, "head": h - 1}
    upper = {"ctx": ctx, "head": h + 1}
    across = [{"ctx": ctx_of(u, x, w), "head": h} for x in xs]
    along = [{"ctx": ctx_of(y, v, w), "head": h} for y in ys]
    partners = [{"ctx": ctx_of(u, v, s), "head": h} for s in ws]

    def at_step(s):
        if s == 0:
            return [(h, None)]
        return [(lows[s], lows[s] >= 0), (highs[s], highs[s] < heads)]

    def column_step(s):
        ops = []
        for place, condition in at_step(s):
            block = block_of(u, v, w, place)
            own = s == 0
            if not own:
                ops.append(wait_for(block, None, condition))
            if own or place is highs[s]:
                ops.append(plan(block, None, down, both(condition, h > 0), own))
            if own or place is lows[s]:
                ops.append(plan(block, None, upper, both(condition, h + 1 < heads), own))
            for target in across + along + partners:
                ops.append(plan(block, None, target, condition, own))
        return ops

    def cross_step(s):
        ops = []
        for place, condition in at_step(s):
            for x in xs:
                block = block_of(u, x, w, place)
                ops.append(wait_for(block, None, condition))
                for target in along:
                    ops.append(plan(block, 0, target, condition))
                for target in partners:
                    ops.append(plan(block, None, target, condition))
            for y in ys:
                block = block_of(y, v, w, place)
                ops.append(wait_for(block, None, condition))
                for target in across:
                    ops.append(plan(block, 1, target, condition))
                for target in partners:
                    ops.append(plan(block, None, target, condition))
        return ops

    def corner_step(s):
        ops = []
        for place, condition in at_step(s):
            for x in xs:
                for y in ys:
                    block = block_of(y, x, w, place)
                    for half in (0, 1):
                        ops.append(wait_for(block, half, condition))
                        for target in partners:
                            ops.append(plan(block, half, target, condition))
        return ops

    def foreign(uu, vv, halves):
        ops = []
        for s in ws:
            for place in range(heads):
                block = block_of(uu, vv, s, place)
                ops += [wait_for(block, half, None) for half in halves]
        return ops

    stages = [[]]
    groups = []
    for s in range(heads):
        stages[0] += column_step(s)
        if s >= 1:
            stages[0] += cross_step(s - 1)
        if s >= 2:
            stages[0] += corner_step(s - 2)
    groups.append((u, v, w))
    for s in ws:
        stages.append(foreign(u, v, (None,)) if s is ws[0] else [])
        groups.append((u, v, s))
    last = cross_step(heads - 1)
    if heads >= 2:
        last += corner_step(heads - 2)
    for x in xs:
        stages.append(last)
        last = []
        groups.append((u, x, w))
    for y in ys:
        stages.append(last)
        last = []
        groups.append((y, v, w))
    for s in ws:
        for x in xs:
            stages.append(foreign(u, x, (None,)) if s is ws[0] else [])
            groups.append((u, x, s))
        for y in ys:
            stages.append(foreign(y, v, (None,)) if s is ws[0] else [])
            groups.append((y, v, s))
    first = True
    for x in xs:
        for y in ys:
            stages.append(corner_step(heads - 1) if first else [])
            first = False
            groups.append((y, x, w))
    for s in ws:
        for x in xs:
            for y in ys:
                stages.append(foreign(y, x, (0, 1)) if s is ws[0] else [])
                groups.append((y, x, s))
    bases = [block_of(*place, 0) for place in groups]

    def perform(ops):
        for op in ops:
            if op[0] == "send":
                index = op[1]
                guarded(sends[index][3], lambda index=index: copy_of(index).start())
            else:
                _, block, half, condition = op

                def wait(block=block, half=half):
                    pltpu.make_async_remote_copy(
                        src_ref=gathered.at[block, span(half)],
                        dst_ref=gathered.at[block, span(half)],
                        send_sem=send_sem.at[0],
                        recv_sem=recv_of(block, half),
                        device_id={"ctx": ctx, "head": h},
                        device_id_type=pl.DeviceIdType.MESH,
                    ).wait_recv()

                guarded(condition, wait)

    gate_copy = pltpu.make_async_copy(gate_hbm, gate_w, weight_sem.at[0])
    up_copy = pltpu.make_async_copy(up_hbm, up_w, weight_sem.at[1])
    own_copy = pltpu.make_async_copy(own_ref, gathered.at[mine], own_sem)

    barrier = pltpu.get_barrier_semaphore()
    for target, condition in peers:
        guarded(
            condition,
            lambda target=target: pl.semaphore_signal(
                barrier, inc=1, device_id=target, device_id_type=pl.DeviceIdType.MESH
            ),
        )
    count = len(peers) - 2 + (h > 0).astype(jnp.int32) + (h + 1 < heads).astype(jnp.int32)
    pl.semaphore_wait(barrier, count)

    slots = heads * capacity
    chunks = width // 128
    row_id = lax.broadcasted_iota(jnp.int32, (rows, rows), 0)
    col_id = lax.broadcasted_iota(jnp.int32, (rows, rows), 1)
    earlier = (row_id < col_id).astype(jnp.bfloat16)
    slot_id = lax.broadcasted_iota(jnp.int32, (capacity, rows), 0)
    note_id = lax.broadcasted_iota(jnp.int32, (extra, 128), 0)

    def load(block, slot):
        return pltpu.make_async_copy(gathered.at[block], block_ref.at[slot], load_sem.at[slot])

    def note_row(slot, note):
        tile = note // 8
        place = pl.multiple_of(lax.rem(tile, chunks) * 128, 128)
        line = (tile // chunks) * 8 + lax.rem(note, 8)
        piece = block_ref[slot, pl.ds(rows, extra), pl.ds(place, 128)].astype(jnp.float32)
        return jnp.sum(jnp.where(note_id == line, piece, 0.0), 0, keepdims=True)

    def compute(base):
        load(base, 0).start()

        def each(i, carry):
            slot = lax.rem(i, 2)
            load(base + i, slot).wait()

            @pl.when(i + 1 < heads)
            def _():
                load(base + i + 1, 1 - slot).start()

            gate = note_row(slot, mine) + note_row(slot, experts + mine)
            wanted = gate > 0.0
            ones = jnp.broadcast_to(wanted.astype(jnp.float32), (16, rows)).astype(jnp.bfloat16)
            rank = jnp.dot(ones, earlier, preferred_element_type=jnp.float32)[0:1].astype(jnp.int32)
            pick = (slot_id == rank) & wanted
            scale = jnp.sum(jnp.where(pick, gate, 0.0), 1, keepdims=True)
            place = pl.multiple_of(i * capacity, 16)
            inputs[pl.ds(place, capacity), :] = jnp.dot(
                pick.astype(jnp.float32).astype(jnp.bfloat16),
                block_ref[slot, pl.ds(0, rows), :],
                preferred_element_type=jnp.float32,
            ).astype(jnp.bfloat16)
            scales[pl.ds(place, capacity), :] = jnp.broadcast_to(scale, (capacity, 128))
            return carry

        lax.fori_loop(0, heads, each, 0)
        hidden_width = gate_w.shape[1]
        step = 256 if hidden_width % 256 == 0 else hidden_width
        given = inputs[...]
        factor = scales[:, 0:1]
        place = pl.ds(pl.multiple_of(base * capacity, 16), slots)
        for n in range(0, hidden_width, step):
            gate = jnp.dot(given, gate_w[:, n : n + step], preferred_element_type=jnp.float32)
            up = jnp.dot(given, up_w[:, n : n + step], preferred_element_type=jnp.float32)
            value = gate / (1.0 + jnp.exp(-gate)) * up * factor
            hidden_ref[place, n : n + step] = value.astype(jnp.bfloat16)

    own_copy.start()
    gate_copy.start()
    up_copy.start()
    perform(stages[0])
    own_copy.wait()
    gate_copy.wait()
    up_copy.wait()

    def stage(t, carry):
        for i in range(1, len(stages)):
            if stages[i]:
                pl.when(t == i)(functools.partial(perform, stages[i]))
        compute(choose(t, bases))
        return carry

    lax.fori_loop(0, len(stages), stage, 0)
    for index in range(len(sends)):
        guarded(sends[index][3], lambda index=index: copy_of(index).wait_send())


def expert_inputs(own, w_gate, w_up, ctx_count, heads, experts, rows, capacity):
    devices = ctx_count * heads
    total, width = own.shape
    hidden_width = w_gate.shape[1]
    return pl.pallas_call(
        functools.partial(expert_kernel, ctx_count, heads, experts, rows, total - rows, capacity),
        in_specs=[pl.BlockSpec(memory_space=pl.ANY)] * 3,
        out_specs=[
            pl.BlockSpec(memory_space=pl.ANY),
            pl.BlockSpec(memory_space=pltpu.VMEM),
        ],
        out_shape=[
            jax.ShapeDtypeStruct((devices, total, width), jnp.bfloat16),
            jax.ShapeDtypeStruct((devices * capacity, hidden_width), jnp.bfloat16),
        ],
        scratch_shapes=[
            pltpu.VMEM(w_gate.shape, jnp.bfloat16),
            pltpu.VMEM(w_up.shape, jnp.bfloat16),
            pltpu.VMEM((2, total, width), jnp.bfloat16),
            pltpu.VMEM((heads * capacity, width), jnp.bfloat16),
            pltpu.VMEM((heads * capacity, 128), jnp.float32),
            pltpu.SemaphoreType.DMA((2,)),
            pltpu.SemaphoreType.DMA((2,)),
            pltpu.SemaphoreType.DMA,
            pltpu.SemaphoreType.DMA((6 * devices,)),
            pltpu.SemaphoreType.DMA((devices,)),
            pltpu.SemaphoreType.DMA((devices,)),
        ],
        compiler_params=pltpu.CompilerParams(collective_id=0, has_side_effects=True),
        name="expert_inputs",
    )(own, w_gate, w_up)


def spread_kernel(per_owner, pick_ref, rows_ref, out_ref):
    owners = out_ref.shape[0]
    width = rows_ref.shape[2]
    for i in range(pick_ref.shape[0]):
        spread = jnp.dot(pick_ref[i], rows_ref[i], preferred_element_type=jnp.float32)
        out_ref[:, i] = spread.astype(out_ref.dtype).reshape(owners, per_owner, width)


def spread_rows(pick, weighted, owners):
    blocks, rows, capacity = pick.shape
    width = weighted.shape[2]
    per_owner = rows // owners
    group = 4
    return pl.pallas_call(
        functools.partial(spread_kernel, per_owner),
        grid=(blocks // group,),
        in_specs=[
            pl.BlockSpec((group, rows, capacity), lambda b: (b, 0, 0)),
            pl.BlockSpec((group, capacity, width), lambda b: (b, 0, 0)),
        ],
        out_specs=pl.BlockSpec((owners, group, per_owner, width), lambda b: (0, b, 0, 0)),
        out_shape=jax.ShapeDtypeStruct((owners, blocks, per_owner, width), jnp.bfloat16),
        name="spread_rows",
    )(pick, weighted)


def attention_kernel(pair, tokens, first_row, q_ref, cos_ref, sin_ref, gain_ref, kv_ref, out_ref, m_ref, a_ref):
    rows_here = q_ref.shape[0]
    here = lax.axis_index("ctx")
    factor = math.log2(math.e) / math.sqrt(HD)
    heads = []
    for i in range(pair):
        lanes = slice(i * HD, (i + 1) * HD)
        raw = q_ref[:, lanes]
        scaled = raw * lax.rsqrt(jnp.mean(raw * raw, -1, keepdims=True) + EPSILON)
        scaled = scaled * (gain_ref[:, lanes] * factor)
        turned = scaled * cos_ref[...] + pltpu.roll(scaled, HD // 2, 1) * sin_ref[...]
        heads.append(turned.astype(jnp.bfloat16))

    def piece(start, length, masked, first):
        keys = kv_ref[pl.ds(start, length), :HD]
        values = kv_ref[pl.ds(start, length), HD:]
        values = jnp.concatenate([values, jnp.ones_like(values)], 1)
        if masked:
            rows = lax.broadcasted_iota(jnp.int32, (rows_here, length), 0) + first_row
            cols = lax.broadcasted_iota(jnp.int32, (rows_here, length), 1)
        for i in range(pair):
            lanes = slice(i * HD, (i + 1) * HD)
            wide = slice(i * 2 * HD, (i + 1) * 2 * HD)
            scores = lax.dot_general(
                heads[i], keys, (((1,), (1,)), ((), ())), preferred_element_type=jnp.float32
            )
            if masked:
                scores = jnp.where(rows >= cols, scores, -1e30)
            top = jnp.max(scores, -1, keepdims=True)
            if first:
                fresh = jnp.broadcast_to(top, (rows_here, HD))
            else:
                old = m_ref[:, lanes]
                fresh = jnp.maximum(old, top)
            weights = jnp.exp2(scores - fresh[:, :1]).astype(jnp.bfloat16)
            part = jnp.dot(weights, values, preferred_element_type=jnp.float32)
            if first:
                a_ref[:, wide] = part
            else:
                decay = jnp.exp2(old - fresh)
                a_ref[:, wide] = a_ref[:, wide] * jnp.concatenate([decay, decay], 1) + part
            m_ref[:, lanes] = fresh

    piece(pl.multiple_of(here * tokens, tokens), first_row + rows_here, True, True)

    def step(j, carry):
        piece(pl.multiple_of(j * tokens, tokens), tokens, False, False)
        return carry

    lax.fori_loop(0, here, step, 0)
    for i in range(pair):
        begin = i * 2 * HD
        out_ref[:, i * HD : (i + 1) * HD] = (
            a_ref[:, begin : begin + HD] / a_ref[:, begin + HD : begin + 2 * HD]
        ).astype(out_ref.dtype)


def attention(queries, cos, sin, gain, kv, part, parts):
    tokens, width = queries.shape
    rows = tokens // parts
    pair = 4
    cols = pair * HD
    work = rows * kv.shape[0] * width
    return pl.pallas_call(
        functools.partial(attention_kernel, pair, tokens, part * rows),
        grid=(width // cols,),
        in_specs=[
            pl.BlockSpec((rows, cols), lambda i: (part, i)),
            pl.BlockSpec((rows, HD), lambda i: (part, 0)),
            pl.BlockSpec((rows, HD), lambda i: (part, 0)),
            pl.BlockSpec((1, cols), lambda i: (0, i)),
            pl.BlockSpec(kv.shape, lambda i: (0, 0)),
        ],
        out_specs=pl.BlockSpec((rows, cols), lambda i: (0, i)),
        out_shape=jax.ShapeDtypeStruct((rows, width), jnp.bfloat16),
        scratch_shapes=[
            pltpu.VMEM((rows, cols), jnp.float32),
            pltpu.VMEM((rows, 2 * cols), jnp.float32),
        ],
        cost_estimate=pl.CostEstimate(
            flops=8 * work, bytes_accessed=4 * rows * width * 2, transcendentals=work // HD
        ),
        name=f"attention_{part}",
    )(queries, cos, sin, gain, kv)


def body(
    branch_rows,
    expert_ids,
    targets,
    router,
    w_gate,
    w_up,
    w_down,
    stream,
    attn_gain,
    q_gain,
    k_gain,
    w_query,
    w_key,
    w_value,
    w_out,
):
    ctx_count = lax.axis_size("ctx")
    head_count = lax.axis_size("head")
    devices = ctx_count * head_count
    experts = router.shape[1]
    rows_here = branch_rows.shape[0]
    top_count = expert_ids.shape[1]
    model_width = branch_rows.shape[1]
    capacity = 3 * rows_here * top_count // (2 * experts)
    local_tokens = stream.shape[0]
    per_owner = rows_here // ctx_count
    ctx_here = lax.axis_index("ctx")
    head_here = lax.axis_index("head")

    owner_ids = targets // local_tokens
    owned = owner_ids[:, None] == jnp.arange(ctx_count, dtype=jnp.int32)[None, :]
    order_in = jnp.sum(
        jnp.where(owned, exclusive_count(owned.astype(jnp.bfloat16)), 0.0), 1
    ).astype(jnp.int32)
    place = owner_ids * per_owner + order_in
    turn = place[None, :] == jnp.arange(rows_here, dtype=jnp.int32)[:, None]
    turn_bf = turn.astype(jnp.bfloat16)
    ordered = jnp.dot(turn_bf, branch_rows, preferred_element_type=jnp.float32).astype(jnp.bfloat16)
    ids = jnp.dot(
        turn_bf, expert_ids.astype(jnp.bfloat16), preferred_element_type=jnp.float32
    ).astype(jnp.int32)
    spots = jnp.sum(jnp.where(turn, (targets % local_tokens)[None, :], 0), 1)
    logits = jnp.dot(ordered, router, preferred_element_type=jnp.float32)
    chosen = jnp.any(
        ids[:, :, None] == jnp.arange(experts, dtype=jnp.int32)[None, None, :], axis=1
    )
    highest = jnp.max(jnp.where(chosen, logits, -jnp.inf), -1, keepdims=True)
    raised = jnp.where(chosen, jnp.exp(jnp.where(chosen, logits - highest, 0.0)), 0.0)
    gates = raised / jnp.sum(raised, -1, keepdims=True)
    gates_high = lax.reduce_precision(gates, 8, 7)
    gates_low = gates - gates_high
    spots_high = (spots // 128).astype(jnp.float32)[:, None]
    spots_low = (spots % 128).astype(jnp.float32)[:, None]
    per_note = jnp.concatenate([gates_high, gates_low, spots_high, spots_low], 1).T
    group_of = 8 * (model_width // 128)
    note_groups = -(-per_note.shape[0] // group_of)
    per_note = jnp.pad(per_note, ((0, note_groups * group_of - per_note.shape[0]), (0, 0)))
    extra = (
        per_note.reshape(note_groups, model_width // 128, 8, rows_here)
        .transpose(0, 2, 1, 3)
        .reshape(note_groups * 8, model_width)
        .astype(jnp.bfloat16)
    )
    padded = -(-capacity // 16) * 16
    gathered, hidden = expert_inputs(
        jnp.concatenate([ordered, extra], 0),
        w_gate[0], w_up[0], ctx_count, head_count, experts, rows_here, padded,
    )

    mine = ctx_here * head_count + head_here
    notes = (
        gathered[:, rows_here:]
        .reshape(devices, note_groups, 8, model_width // 128, rows_here)
        .transpose(0, 1, 3, 2, 4)
        .reshape(devices, note_groups * group_of, rows_here)
        .astype(jnp.float32)
    )
    note_ids = jnp.arange(note_groups * group_of, dtype=jnp.int32)[:, None]
    my_gate = jnp.sum(
        jnp.where((note_ids == mine) | (note_ids == experts + mine), notes, 0.0), 1
    )
    wanted = my_gate > 0.0
    rank = exclusive_count(wanted.astype(jnp.bfloat16)[:, :, None])[:, :, 0].astype(jnp.int32)
    back_bf = (
        (rank[:, :, None] == jnp.arange(padded, dtype=jnp.int32)[None, None, :])
        & wanted[:, :, None]
    ).astype(jnp.bfloat16)
    weighted = jnp.dot(hidden, w_down[0], preferred_element_type=jnp.float32).astype(jnp.bfloat16)
    shares = spread_rows(
        back_bf, weighted.reshape(devices, padded, model_width), ctx_count
    ).reshape(devices * rows_here, model_width)
    landed = lax.psum_scatter(shares, "ctx", scatter_dimension=0, tiled=True)
    landed = lax.psum_scatter(landed, "head", scatter_dimension=1, tiled=True)

    spots_all = (notes[:, 2 * experts] * 128.0 + notes[:, 2 * experts + 1]).reshape(
        devices, ctx_count, per_owner
    )
    spot_ids = (
        lax.dynamic_index_in_dim(spots_all, ctx_here, 1, keepdims=False).astype(jnp.int32).reshape(-1)
    )
    aimed = (
        jnp.arange(local_tokens, dtype=jnp.int32)[:, None] == spot_ids[None, :]
    ).astype(jnp.bfloat16)
    joined = (
        stream.astype(jnp.float32) + jnp.dot(aimed, landed, preferred_element_type=jnp.float32)
    ).astype(jnp.bfloat16)
    full_rows = lax.all_gather(joined, "head", axis=1, tiled=True)
    full_float = full_rows.astype(jnp.float32)
    normed = (
        full_float
        * lax.rsqrt(jnp.mean(full_float * full_float, -1, keepdims=True) + EPSILON)
        * attn_gain
    ).astype(jnp.bfloat16)
    per_device = w_query.shape[1] // HD
    kv_head = head_here * per_device // (QH // KVH)
    positions = ctx_here * local_tokens + jnp.arange(local_tokens, dtype=jnp.int32)
    cos, sin = rotary_tables(positions)
    key_value = jnp.concatenate(
        [
            lax.dynamic_slice_in_dim(w_key, kv_head * HD, HD, 1),
            lax.dynamic_slice_in_dim(w_value, kv_head * HD, HD, 1),
        ],
        1,
    )
    key_scales = lax.dynamic_slice_in_dim(k_gain, kv_head * HD, HD, 0)
    kv_rows = jnp.dot(normed, key_value, preferred_element_type=jnp.float32)
    keys = kv_rows[:, :HD]
    keys = keys * lax.rsqrt(jnp.mean(keys * keys, -1, keepdims=True) + EPSILON) * key_scales
    keys = keys * cos + jnp.roll(keys, HD // 2, 1) * sin
    kv = lax.all_gather(
        jnp.concatenate([keys, kv_rows[:, HD:]], 1).astype(jnp.bfloat16), "ctx", axis=0, tiled=True
    )
    queries = jnp.dot(normed, w_query, preferred_element_type=jnp.float32)
    parts = 2
    rows_part = local_tokens // parts
    sums = []
    for part in range(parts):
        attended = attention(queries, cos, sin, q_gain.reshape(1, -1), kv, part, parts)
        partial_out = jnp.dot(attended, w_out, preferred_element_type=jnp.float32)
        summed = lax.psum_scatter(
            partial_out.astype(jnp.bfloat16), "head", scatter_dimension=1, tiled=True
        )
        sums.append(
            joined[part * rows_part : (part + 1) * rows_part].astype(jnp.float32)
            + summed.astype(jnp.float32)
        )
    return jnp.concatenate(sums, 0).astype(jnp.bfloat16)


def solution(mesh):
    in_specs = (
        P(("ctx", "head"), None),
        P(("ctx", "head"), None),
        P(("ctx", "head")),
        P(),
        P(("ctx", "head"), None, None),
        P(("ctx", "head"), None, None),
        P(("ctx", "head"), None, None),
        P("ctx", "head"),
        P(),
        P("head"),
        P(),
        P(None, "head"),
        P(),
        P(),
        P("head", None),
    )
    out_specs = P("ctx", "head")
    return jax.shard_map(body, mesh=mesh, in_specs=in_specs, out_specs=out_specs, check_vma=False)
```
